128 devices in a mesh: dp: 8 (over z_hi, y), ty: 4 (over z_lo, core), tz: 4 (over x).
Axes of the slice: x: 4, y: 4, z: 4 (z_hi: 2, z_lo: 2; z = z_hi * 2 + z_lo), core: 2. Of those that a mesh axis runs over, the one named last changes fastest.
Arguments:
- inputs: bfloat16 [8, 4, 48, 48, 256], P('dp', None, 'ty', 'tz'), may hold values from -6 to 6
- pre_first: bfloat16 [8, 4, 48, 48, 256], P('dp', None, 'ty', 'tz'), may hold values from -6 to 6
- pre_second: bfloat16 [8, 4, 48, 48, 256], P('dp', None, 'ty', 'tz'), may hold values from -6 to 6
- grad_out: bfloat16 [8, 4, 48, 48, 256], P('dp', None, 'ty', 'tz'), may hold values from -6 to 6
- w_first: bfloat16 [256, 27, 256], P('dp'), may hold values from -0.078125 to 0.078125
- w_second: bfloat16 [256, 27, 256], P('dp'), may hold values from -0.078125 to 0.078125
Outputs:
- grad_input: bfloat16 [8, 4, 48, 48, 256], P('dp', None, 'ty', 'tz')
- grad_w_first: float32 [256, 27, 256], P('dp')
- grad_w_second: float32 [256, 27, 256], P('dp')
The draws below stay inside these ranges and needn't reach their ends.
All inputs are finite; a program needn't handle non-finite values.
Results may differ from the reference program's by a relative error of at most 0.0049.
Values may be sent and summed in bfloat16 or wider, within the bound.
No kernel may reach another device: no remote copies, remote signals or barrier semaphores. Data moves between devices by JAX's collectives and lax.ppermute only.
A program may use at most 128 MiB of HBM per device.

```python
import math
import jax
import jax.numpy as jnp
from jax import lax

C = 256
TAPS = 27
DX = 4
NY = 48
NZ = 48
FRAMES = 8


def strengthened(result, own_key, source, target, blocks, factor):
    def block_of(position):
        return (jnp.arange(result.shape[position]) // (result.shape[position] // blocks)).reshape((-1,) + (1,) * (result.ndim - 1 - position))

    near = jax.random.permutation(own_key, blocks)[block_of(target)]
    other_side = (block_of(target) + blocks // 2) % blocks
    return jnp.where((block_of(source) == near) | (block_of(source) == other_side), factor * result, result)


def levels(own_key, extent, pieces, smallest, high):
    gain = 1.0
    for axis_at, parts in pieces:
        steps = jax.random.uniform(jax.random.fold_in(jax.random.fold_in(own_key, 6), axis_at), (parts,), jnp.float32, smallest / len(pieces), high / len(pieces))
        gain = gain * jnp.repeat(jnp.exp(steps), extent[axis_at] // parts).reshape((-1,) + (1,) * (len(extent) - 1 - axis_at))
    return gain


def noise(stream_key, dims, scale, limit, shards=(), kind=jnp.bfloat16):
    array = scale * jax.random.normal(stream_key, dims, jnp.float32)
    if shards:
        array = array * levels(stream_key, dims, shards, -0.22, 0.18)
    return jnp.clip(array, -limit, limit).astype(kind)


def gaussian_with(key, dims, scale, most, pieces, heavy, kind=jnp.bfloat16):
    values = scale * jax.random.normal(key, dims, jnp.float32)
    if pieces:
        values = values * levels(key, dims, pieces, -0.22, 0.18)
    return jnp.clip(strengthened(values, jax.random.fold_in(key, 3), *heavy), -most, most).astype(kind)


def setup_inputs(seed: int = 0) -> dict:
    streams_of = jax.random.split(jax.random.key(seed), 7)
    inputs = gaussian_with(streams_of[0], (FRAMES, DX, NY, NZ, C), 1.0, 6.0, ((0, 8), (2, 4), (3, 4)), (0, 4, 8, 2.0))
    pre_first = gaussian_with(streams_of[1], (FRAMES, DX, NY, NZ, C), 1.0, 6.0, ((0, 8), (2, 4), (3, 4)), (0, 4, 8, 2.0))
    pre_second = noise(streams_of[2], (FRAMES, DX, NY, NZ, C), 1.0, 6.0, ((0, 8), (2, 4), (3, 4)))
    grad_out = noise(streams_of[3], (FRAMES, DX, NY, NZ, C), 1.0, 6.0, ((0, 8), (2, 4), (3, 4)))
    w_first = noise(streams_of[4], (C, TAPS, C), (TAPS * C) ** -0.5, 0.078125, ((0, 8),))
    w_second = noise(streams_of[5], (C, TAPS, C), (TAPS * C) ** -0.5, 0.078125, ((0, 8),))
    return {"inputs": inputs, "pre_first": pre_first, "pre_second": pre_second, "grad_out": grad_out, "w_first": w_first, "w_second": w_second}


def make_offsets():
    return [(shift_a, shift_b, shift_c) for shift_a in (-1, 0, 1) for shift_b in (-1, 0, 1) for shift_c in (-1, 0, 1)]

def pad_space(field):
    return jnp.pad(field, ((0, 0), (1, 1), (1, 1), (1, 1), (0, 0)))

def window(padded, offset, shape):
    return padded[:, 1 + offset[0]:1 + offset[0] + shape[1], 1 + offset[1]:1 + offset[1] + shape[2], 1 + offset[2]:1 + offset[2] + shape[3], :]

def data_grad(grad, weight):
    shape = grad.shape
    width = shape[4]
    padded = pad_space(grad)
    total = jnp.zeros((shape[0] * shape[1] * shape[2] * shape[3], weight.shape[0]), jnp.float32)
    for index, offset in enumerate(make_offsets()):
        back = (-offset[0], -offset[1], -offset[2])
        piece = window(padded, back, shape).reshape(-1, width)
        total = total + lax.dot_general(piece, weight[:, index, :], (((1,), (1,)), ((), ())), preferred_element_type=jnp.float32)
    return total.reshape(shape[0], shape[1], shape[2], shape[3], -1)

def weight_grad(act, grad):
    shape = act.shape
    padded = pad_space(act)
    flat_grad = grad.reshape(-1, grad.shape[4])
    terms = []
    for index, offset in enumerate(make_offsets()):
        piece = window(padded, offset, shape).reshape(-1, shape[4])
        terms.append(lax.dot_general(piece, flat_grad, (((0,), (0,)), ((), ())), preferred_element_type=jnp.float32))
    return jnp.stack(terms, axis=1)

def reference(inputs, pre_first, pre_second, grad_out, w_first, w_second):
    shape = inputs.shape
    scale = 1.0 / math.sqrt(shape[0] * shape[1] * shape[2] * shape[3])
    grad_top = jnp.where(pre_second > 0, grad_out, jnp.zeros((), jnp.bfloat16))
    active = jnp.where(pre_first > 0, pre_first, jnp.zeros((), jnp.bfloat16))
    upstream = data_grad(grad_top, w_second)
    grad_low = jnp.where(pre_first > 0, upstream, jnp.zeros((), jnp.float32)).astype(jnp.bfloat16)
    grad_w_second = weight_grad(active, grad_top) * scale
    grad_w_first = weight_grad(inputs, grad_low) * scale
    grad_input = data_grad(grad_low, w_first).astype(jnp.bfloat16)
    return (grad_input, grad_w_first, grad_w_second)
```

```python
import math

import jax
import jax.numpy as jnp
from jax import lax
from jax.sharding import Mesh
from jax.sharding import PartitionSpec as P


AXES = ("zhi", "y", "zlo", "core", "x")
SIZES = (2, 4, 2, 2, 4)
BF = jnp.bfloat16
F32 = jnp.float32


def flat(zhi, y, zlo, core, x):
    return (((zhi * 4 + y) * 2 + zlo) * 2 + core) * 4 + x


def pairs(move):
    out = []
    for zhi in range(2):
        for y in range(4):
            for zlo in range(2):
                for core in range(2):
                    for x in range(4):
                        out.append((flat(zhi, y, zlo, core, x), flat(*move(zhi, y, zlo, core, x))))
    return out


def send(value, move):
    return lax.ppermute(value, AXES, pairs(move))


def x_by(step):
    return lambda zhi, y, zlo, core, x: (zhi, y, zlo, core, (x + step) % 4)


def core_swap(zhi, y, zlo, core, x):
    return (zhi, y, zlo, 1 - core, x)


def zlo_swap(zhi, y, zlo, core, x):
    return (zhi, y, 1 - zlo, core, x)


def turned(zhi, y, zlo, core, x):
    return (core, x, zlo, zhi, y)


def rows_of(field):
    return field[0].transpose(1, 2, 0, 3).reshape(144, 1024)


def blocks_of_channels(rows):
    return rows.reshape(144, 4, 8, 32).transpose(2, 0, 1, 3).reshape(8, 144, 128)


def region(own, other, core):
    lanes = own[0].shape[1]
    a = jnp.concatenate([t.reshape(12, 12, lanes) for t in own], axis=1)
    b = jnp.concatenate([t.reshape(12, 12, lanes) for t in other], axis=1)
    first = core == 0
    return jnp.concatenate([jnp.where(first, a, b), jnp.where(first, b, a)], axis=0)


def edged(field, zlo, width):
    low = zlo == 0
    mine = jnp.where(low, field[24 - width :], field[:width])
    got = send(mine, zlo_swap)
    zero = jnp.zeros_like(got)
    return jnp.concatenate([jnp.where(low, zero, got), field, jnp.where(low, got, zero)], axis=0)


def z_shift(field, c, z_at):
    if c == 0:
        return field
    source = z_at - c
    ok = ((source >= 0) & (source < 48))[None, :, None]
    return jnp.where(ok, jnp.roll(field, c, axis=1), jnp.zeros((), field.dtype))


def banded(shard):
    taps = shard.transpose(1, 0, 2).reshape(3, 9, 32, 256)
    zero = jnp.zeros((9, 32, 256), shard.dtype)
    columns = []
    for xs in range(4):
        columns.append(
            jnp.stack([taps[x - xs + 1] if abs(x - xs) <= 1 else zero for x in range(4)], axis=1)
        )
    return jnp.concatenate(columns, axis=-1).reshape(1152, 1024)


def data_grad(field, bands, z_at):
    n = field.shape[0]
    prod = lax.dot_general(
        field.reshape(n * 48, 1024), bands, (((1,), (1,)), ((), ())), preferred_element_type=F32
    ).reshape(n, 48, 9, 128)
    total = None
    for c in (-1, 0, 1):
        part = None
        for b in (-1, 0, 1):
            term = prod[1 - b : 1 - b + n - 2, :, 3 * (b + 1) + (c + 1)]
            part = term if part is None else part + term
        part = z_shift(part, c, z_at)
        total = part if total is None else total + part
    return total


def shifted(field, sign, z_at):
    cols = []
    for b in (-1, 0, 1):
        for c in (-1, 0, 1):
            moved = z_shift(field, -sign * c, z_at)
            cols.append(moved[1 + sign * b : 25 + sign * b])
    return jnp.concatenate(cols, axis=-1).reshape(1152, 1152)


def filter_grad(small, large, sign):
    prod = lax.dot_general(
        small, large, (((0,), (0,)), ((), ())), preferred_element_type=F32
    ).reshape(9, 4, 32, 4, 256)
    out = []
    for a in (-1, 0, 1):
        total = None
        for xs in range(4):
            xl = xs - sign * a
            if 0 <= xl < 4:
                term = prod[:, xs, :, xl]
                total = term if total is None else total + term
        out.append(total)
    return jnp.concatenate(out, axis=0)


def from_x(value_for):
    return [value_for(0)] + [send(value_for(4 - r), x_by(4 - r)) for r in (1, 2, 3)]


def local(inputs, pre_first, pre_second, grad_out, w_first, w_second):
    zlo, core, x = lax.axis_index("zlo"), lax.axis_index("core"), lax.axis_index("x")
    scale = 1.0 / math.sqrt(8 * 4 * 48 * 48)
    zero = jnp.zeros((), BF)
    z_rel = (jnp.arange(48) + 12 * x) % 48
    z_abs = jnp.arange(48)

    top = rows_of(jnp.where(pre_second > 0, grad_out, zero))
    act = blocks_of_channels(rows_of(jnp.where(pre_first > 0, pre_first, zero)))
    inp = rows_of(inputs)

    act2 = act.reshape(2, 4, 144, 128)

    def act_for(r):
        return lax.dynamic_index_in_dim(act2, (x + r) % 4, 1, keepdims=False)

    def load_for(r):
        blocks = act_for(r)
        return jnp.concatenate([top, blocks[0], blocks[1]], axis=-1)

    w2 = send(w_second, turned)
    got = from_x(load_for)
    w1 = send(w_first, turned)
    inp_x = from_x(lambda r: inp)

    first = core == 0
    stack = jnp.stack(got)
    tops = stack[:, :, :1024]
    mine = jnp.where(first, stack[:, :, 1024:1152], stack[:, :, 1152:])
    away = jnp.where(first, stack[:, :, 1152:], stack[:, :, 1024:1152])
    swapped = send(jnp.concatenate([tops, away], axis=-1), core_swap)
    top_reg = region([tops[r] for r in range(4)], [swapped[r, :, :1024] for r in range(4)], core)
    act_reg = region([mine[r] for r in range(4)], [swapped[r, :, 1024:] for r in range(4)], core)
    both = edged(jnp.concatenate([top_reg, act_reg], axis=-1), zlo, 2)
    top_pad = both[:, :, :1024]
    act_pad = both[1:27, :, 1024:]

    low = jnp.where(act_pad > 0, data_grad(top_pad, banded(w2), z_rel), jnp.zeros((), F32)).astype(BF)

    inp_sw = send(jnp.stack(inp_x), core_swap)
    inp_reg = region(inp_x, [inp_sw[r] for r in range(4)], core)

    low_abs = lax.dynamic_slice_in_dim(
        jnp.concatenate([low, low], axis=1), (48 - 12 * x) % 48, 48, axis=1
    )
    low_x = from_x(lambda r: low_abs)
    low_sw = send(jnp.stack(low_x), core_swap)
    low_full = jnp.concatenate(low_x + [low_sw[r] for r in range(4)], axis=-1)

    grad_w2 = filter_grad(shifted(act_pad, 1, z_rel), top_reg.reshape(1152, 1024), 1) * scale
    grad_w1 = filter_grad(shifted(low, -1, z_rel), inp_reg.reshape(1152, 1024), -1) * scale

    lane = jnp.arange(256)
    block = lane // 32
    source = ((block // 4 + core) % 2) * 128 + ((block % 4 + x) % 4) * 32 + lane % 32
    order = (lane[:, None] == source[None, :]).astype(BF)
    w1o = lax.dot_general(
        w1.reshape(864, 256), order, (((1,), (0,)), ((), ())), preferred_element_type=F32
    ).astype(BF)
    bands1 = banded(w1o.reshape(32, 27, 256))
    bands1 = bands1.reshape(1152, 4, 8, 32).transpose(0, 2, 1, 3).reshape(1152, 1024)
    gin = data_grad(low_full, bands1, z_abs).astype(BF)
    gin = gin.reshape(2, 12, 4, 12, 128).transpose(0, 2, 1, 3, 4).reshape(8, 144, 128)
    gin = lax.all_to_all(gin, ("core", "x"), 0, 0, tiled=True)
    gin = gin.reshape(8, 144, 4, 32).transpose(1, 2, 0, 3).reshape(12, 12, 4, 256)
    grad_input = gin.transpose(2, 0, 1, 3)[None]

    flat2 = jnp.pad(grad_w2.reshape(864, 256), ((0, 32), (0, 0))).astype(BF).reshape(16, 56, 256)
    flat1 = jnp.pad(grad_w1.reshape(864, 256).T, ((0, 0), (0, 32))).astype(BF).reshape(16, 16, 896)
    deep = ("zhi", "y", "zlo")
    sum2 = lax.all_to_all(flat2, deep, 0, 0, tiled=True).astype(F32).sum(0).astype(BF)
    sum1 = lax.all_to_all(flat1, deep, 0, 0, tiled=True).astype(F32).sum(0).astype(BF)
    sum2 = send(sum2, turned)
    piece = jnp.concatenate([sum2.reshape(-1), sum1.reshape(-1)]).reshape(224, 128)

    low_side = zlo == 0
    other = send(piece, zlo_swap)
    pair = jnp.stack([jnp.where(low_side, piece, other), jnp.where(low_side, other, piece)])
    xs = jnp.stack(from_x(lambda r: pair))
    xs = jnp.roll(xs, x, axis=0)
    co = send(xs, core_swap)
    all_ = jnp.stack([jnp.where(first, xs, co), jnp.where(first, co, xs)]).reshape(8, 2, 224, 128)
    out2 = all_[:, :, :112].reshape(16 * 56, 256)[:864].reshape(27, 32, 256)
    out1 = all_[:, :, 112:].reshape(8, 2, 16, 896)[..., :864].reshape(8, 32, 27, 32)
    out1 = out1.transpose(1, 2, 0, 3).reshape(32, 27, 256)
    return (grad_input, out1.astype(F32), out2.transpose(1, 0, 2).astype(F32))


def solution(mesh):
    fine = Mesh(mesh.devices.reshape(SIZES), AXES)
    dp, ty = ("zhi", "y"), ("zlo", "core")
    vol = P(dp, None, ty, "x", None)
    filt = P(dp, None, None)
    return jax.shard_map(
        local,
        mesh=fine,
        in_specs=(vol, vol, vol, vol, filt, filt),
        out_specs=(vol, filt, filt),
        check_vma=False,
    )
```

```python
import functools
import math

import jax
import jax.numpy as jnp
from jax import lax
from jax.experimental import pallas as pl
from jax.experimental.pallas import tpu as pltpu
from jax.sharding import Mesh
from jax.sharding import PartitionSpec as P


AXES = ("zhi", "y", "zlo", "core", "x")
SIZES = (2, 4, 2, 2, 4)
BF = jnp.bfloat16
F32 = jnp.float32


def flat(zhi, y, zlo, core, x):
    return (((zhi * 4 + y) * 2 + zlo) * 2 + core) * 4 + x


def pairs(move):
    out = []
    for zhi in range(2):
        for y in range(4):
            for zlo in range(2):
                for core in range(2):
                    for x in range(4):
                        out.append((flat(zhi, y, zlo, core, x), flat(*move(zhi, y, zlo, core, x))))
    return out


def send(value, move):
    return lax.ppermute(value, AXES, pairs(move))


def x_by(step):
    return lambda zhi, y, zlo, core, x: (zhi, y, zlo, core, (x + step) % 4)


def core_swap(zhi, y, zlo, core, x):
    return (zhi, y, zlo, 1 - core, x)


def zlo_swap(zhi, y, zlo, core, x):
    return (zhi, y, 1 - zlo, core, x)


def turned(zhi, y, zlo, core, x):
    return (core, x, zlo, zhi, y)


def rows_of(field):
    return field[0].transpose(1, 2, 0, 3).reshape(144, 1024)


def scalars():
    return jnp.stack([lax.axis_index(n).astype(jnp.int32) for n in ("core", "x", "zlo")])


def iota(shape, dim):
    return lax.broadcasted_iota(jnp.int32, shape, dim)


def spread_matrix(rows, cols):
    r = iota((rows, cols), 0)
    z = r % 16 - 2
    hit = (iota((rows, cols), 1) == 12 * (r // 16) + z) & (z >= 0) & (z < 12)
    return jnp.where(hit, 1.0, 0.0).astype(BF)


def mm(a, b, dims):
    return lax.dot_general(a, b, (dims, ((), ())), preferred_element_type=F32)


def lanes_of(ref, first, count, rows):
    return jnp.concatenate([ref[first + n, :rows, :] for n in range(count)], axis=-1)


def fill_bands(bands, w_ref):
    for bc in range(9):
        for x in range(4):
            for xs in range(4):
                at = (slice(bc * 128 + 32 * x, bc * 128 + 32 * x + 32), slice(256 * xs, 256 * xs + 256))
                if abs(x - xs) <= 1:
                    bands[at] = w_ref[9 * (x - xs + 1) + bc]
                else:
                    bands[at] = jnp.zeros((32, 256), BF)


def z_sum(prod):
    return prod[:, 128:256] + pltpu.roll(prod[:, 256:384], 1, 0) + pltpu.roll(prod[:, :128], prod.shape[0] - 1, 0)


def z_joined(tiles, rr, x, low_row, high_row):
    here, after, before = tiles[rr], tiles[(rr + 1) % 4], tiles[(rr + 3) % 4]
    n = here.shape[0]
    z_tile = (x + rr) % 4
    row = iota(here.shape, 0) % 16
    here = here + jnp.where((row == high_row) & (z_tile != 3), pltpu.roll(after, 12, 0), 0.0)
    return here + jnp.where((row == low_row) & (z_tile != 0), pltpu.roll(before, n - 12, 0), 0.0)


def low_kernel(at, w_ref, o0, o1, o2, o3, p0, p1, p2, p3, low_ref, act_ref, bands, acc, act):
    core, x, zlo = at[0], at[1], at[2]
    fill_bands(bands, w_ref)
    acc[...] = jnp.zeros_like(acc)
    act[...] = jnp.zeros_like(act)
    spread = spread_matrix(224, 168)
    edge_y = jnp.where(zlo == 0, 24, -2)
    edge_a = jnp.where(zlo == 0, 25, 0)
    for rr, pair in enumerate(((o0, p0), (o1, p1), (o2, p2), (o3, p3))):
        for s, ref in enumerate(pair):
            tile = core if s == 0 else 1 - core
            field = mm(spread, lanes_of(ref, 0, 8, 168), ((1,), (0,))).astype(BF)
            for b in (-1, 0, 1):
                prod = mm(field, bands[384 * (b + 1) : 384 * (b + 2), :], ((1,), (1,)))
                part = z_sum(prod)
                rows = pl.ds(pl.multiple_of((12 * tile + b + 3) * 16, 16), 192)
                acc[rr, rows, :] += part[:192]
                rows = pl.ds(pl.multiple_of((edge_y + b + 3) * 16, 16), 32)
                acc[rr, rows, :] += part[192:]
            mine = mm(spread, ref[8 + core], ((1,), (0,)))
            act[rr, pl.ds(pl.multiple_of((12 * tile + 1) * 16, 16), 192), :] += mine[:192]
            rows = pl.ds(pl.multiple_of(edge_a * 16, 16), 16)
            act[rr, rows, :] += jnp.where(zlo == 0, mine[192:208], mine[208:224])
    tiles = [acc[rr, 32:448, :] for rr in range(4)]
    for rr in range(4):
        value = z_joined(tiles, rr, x, 2, 13)
        here = act[rr]
        low_ref[rr] = jnp.where(here > 0, value, 0.0).astype(BF)
        act_ref[rr] = here.astype(BF)


def call(kernel, out_shape, scratch, flops, args, **extra):
    specs = [pl.BlockSpec(memory_space=pltpu.SMEM)] + [pl.BlockSpec(memory_space=pltpu.VMEM)] * (len(args) - 1)
    many = isinstance(out_shape, (list, tuple))
    total = sum(a.size * a.dtype.itemsize for a in args)
    return pl.pallas_call(
        kernel,
        out_shape=out_shape,
        in_specs=specs,
        out_specs=[pl.BlockSpec(memory_space=pltpu.VMEM)] * len(out_shape) if many else pl.BlockSpec(memory_space=pltpu.VMEM),
        scratch_shapes=scratch,
        cost_estimate=pl.CostEstimate(flops=flops, bytes_accessed=total, transcendentals=0),
        compiler_params=pltpu.CompilerParams(vmem_limit_bytes=56 << 20),
        **extra,
    )(*args)


def low_call(at, w, own, other):
    shape = jax.ShapeDtypeStruct((4, 416, 128), BF)
    scratch = [pltpu.VMEM((1152, 1024), BF), pltpu.VMEM((4, 480, 128), F32), pltpu.VMEM((4, 416, 128), F32)]
    return call(low_kernel, [shape, shape], scratch, 4 * 10**9, [at, w, *own, *other])


def filter_kernel(sign, scale, turn, at, s_ref, o0, o1, o2, o3, p0, p1, p2, p3, out_ref, filled, shifts, total):
    core, x = at[0], at[1]
    tiles = [s_ref[rr].astype(F32) for rr in range(4)]
    for rr in range(4):
        filled[rr] = z_joined(tiles, rr, x, 1, 14).astype(BF)
    q = iota((432, 192), 0)
    n = q % 144
    c = q // 144 - 1
    pick = jnp.where(iota((432, 192), 1) == 16 * (n // 12) + 2 + n % 12 + sign * c, 1.0, 0.0).astype(BF)
    pieces = ((o0, p0), (o1, p1), (o2, p2), (o3, p3))
    for rr in range(4):
        for s in range(2):
            tile = core if s == 0 else 1 - core
            windows = [
                filled[rr, pl.ds(pl.multiple_of((12 * tile + 1 + sign * b) * 16, 16), 192), :] for b in (-1, 0, 1)
            ]
            moved = mm(pick, jnp.concatenate(windows, axis=-1), ((1,), (0,))).astype(BF)
            base = (2 * rr + s) * 144
            for b in range(3):
                for c in range(3):
                    shifts[base : base + 144, 128 * (3 * b + c) : 128 * (3 * b + c + 1)] = moved[
                        144 * c : 144 * c + 144, 128 * b : 128 * b + 128
                    ]
    total[...] = jnp.zeros_like(total)
    for xl in range(4):
        large = jnp.concatenate([lanes_of(ref, 2 * xl, 2, 144) for pair in pieces for ref in pair], axis=0)
        for b in range(3):
            prod = mm(shifts[:, 384 * b : 384 * b + 384], large, ((0,), (0,)))
            for a in range(3):
                xs = xl + sign * (a - 1)
                if 0 <= xs < 4:
                    for c in range(3):
                        row = 32 * (9 * a + 3 * b + c)
                        total[row : row + 32, :] += prod[128 * c + 32 * xs : 128 * c + 32 * xs + 32, :]
    result = total[...] * scale
    if turn:
        out_ref[...] = result.T.astype(BF)
    else:
        out_ref[...] = result.astype(BF)


def filter_call(sign, scale, turn, at, small, own, other):
    shape = jax.ShapeDtypeStruct((256, 896) if turn else (896, 256), BF)
    scratch = [pltpu.VMEM((4, 416, 128), BF), pltpu.VMEM((1152, 1152), BF), pltpu.VMEM((896, 256), F32)]
    kernel = functools.partial(filter_kernel, sign, scale, turn)
    return call(kernel, shape, scratch, 3 * 10**9, [at, small, *own, *other])


def lane_target(at, shape, dim):
    r = iota(shape, dim)
    piece, xd, i = r // 128, (r // 32) % 4, r % 32
    j = ((at[0] + piece // 4) % 2) * 4 + (at[1] + piece % 4) % 4
    return 256 * xd + 32 * j + i


def bands_kernel(at, w_ref, out_ref, bands):
    fill_bands(bands, w_ref)
    for piece in range(4):
        shape = (1024, 256)
        r = iota(shape, 1) + 256 * piece
        p, xd, i = r // 128, (r // 32) % 4, r % 32
        j = ((at[0] + p // 4) % 2) * 4 + (at[1] + p % 4) % 4
        order = jnp.where(iota(shape, 0) == 256 * xd + 32 * j + i, 1.0, 0.0).astype(BF)
        out_ref[:, 256 * piece : 256 * piece + 256] = mm(bands[...], order, ((1,), (0,))).astype(BF)


def bands_call(at, w):
    shape = jax.ShapeDtypeStruct((1152, 1024), BF)
    return call(bands_kernel, shape, [pltpu.VMEM((1152, 1024), BF)], 24 * 10**8, [at, w])


def input_kernel(at, bands, o0, o1, o2, o3, p0, p1, p2, p3, out_ref, acc):
    x = at[1]
    order = (o0, o1, o2, o3, p0, p1, p2, p3)
    for rr in range(4):
        field = jnp.concatenate([ref[(rr - n % 4) % 4] for n, ref in enumerate(order)], axis=-1)
        total = None
        for b in (-1, 0, 1):
            part = z_sum(mm(field, bands[384 * (b + 1) : 384 * (b + 2), :], ((1,), (1,))))
            part = part[(1 - b) * 16 : (1 - b) * 16 + 384]
            total = part if total is None else total + part
        acc[rr] = total
    tiles = [acc[rr] for rr in range(4)]
    for rr in range(4):
        out_ref[rr] = z_joined(tiles, rr, x, 2, 13).astype(BF)


def input_call(at, bands, own, other):
    shape = jax.ShapeDtypeStruct((4, 384, 128), BF)
    return call(input_kernel, shape, [pltpu.VMEM((4, 384, 128), F32)], 4 * 10**9, [at, bands, *own, *other])


def place_kernel(at, own, other, out_ref):
    field = jnp.concatenate([own[n] for n in range(4)] + [other[n] for n in range(4)], axis=-1)
    q = iota((144, 192), 0)
    pick = jnp.where(iota((144, 192), 1) == 16 * (q // 12) + 2 + q % 12, 1.0, 0.0).astype(BF)
    field = mm(pick, field, ((1,), (0,))).astype(BF)
    for xd in range(4):
        shape = (1024, 256)
        hit = lane_target(at, shape, 0) == iota(shape, 1) + 256 * xd
        order = jnp.where(hit, 1.0, 0.0).astype(BF)
        out_ref[xd] = mm(field, order, ((1,), (0,))).astype(BF)


def place_call(at, own, other):
    shape = jax.ShapeDtypeStruct((4, 144, 256), BF)
    return call(place_kernel, shape, [], 3 * 10**8, [at, own, other])

def from_x(value_for):
    return [value_for(0)] + [send(value_for(4 - r), x_by(4 - r)) for r in (1, 2, 3)]


def edge_pairs():
    return [
        (flat(zhi, y, zlo, 1 - zlo, x), flat(zhi, y, 1 - zlo, zlo, x))
        for zhi in range(2)
        for y in range(4)
        for zlo in range(2)
        for x in range(4)
    ]


def rows_for_me(shard):
    parts = []
    for step in range(4):
        moves = [
            (flat(zhi, x, zlo, core, x), flat(core, (x + step) % 4, zlo, zhi, x))
            for zhi in range(2)
            for zlo in range(2)
            for core in range(2)
            for x in range(4)
        ]
        parts.append(lax.ppermute(shard, AXES, moves))
    return parts[0] + parts[1] + parts[2] + parts[3]


def local(inputs, pre_first, pre_second, grad_out, w_first, w_second):
    zlo, core, x = lax.axis_index("zlo"), lax.axis_index("core"), lax.axis_index("x")
    at = scalars()
    scale = 1.0 / math.sqrt(8 * 4 * 48 * 48)
    zero = jnp.zeros((), BF)
    first = core == 0

    top = rows_of(jnp.where(pre_second > 0, grad_out, zero)).reshape(144, 8, 128).transpose(1, 0, 2)
    act = rows_of(jnp.where(pre_first > 0, pre_first, zero))
    act = act.reshape(144, 4, 8, 32).transpose(2, 0, 1, 3).reshape(8, 144, 128)
    inp = rows_of(inputs).reshape(144, 8, 128).transpose(1, 0, 2)
    taps1 = w_first.transpose(1, 0, 2)
    taps2 = w_second.transpose(1, 0, 2)

    both = jnp.concatenate([top, act], axis=0)
    edge = jnp.where(zlo == 0, both[:, 120:144], both[:, 0:24])
    edge = lax.ppermute(edge, AXES, edge_pairs())
    both = jnp.concatenate([both, edge], axis=1)

    def load_for(r):
        n = (x + r) % 4
        a = lax.dynamic_index_in_dim(both[8:12], n, 0)
        b = lax.dynamic_index_in_dim(both[12:16], n, 0)
        return jnp.concatenate([both[:8], a, b], axis=0)

    w2 = rows_for_me(taps2)
    load = from_x(load_for)
    load_sw = [send(v, core_swap) for v in load]
    inp, _ = lax.optimization_barrier((inp, load[1]))
    inp_x = from_x(lambda r: inp)
    inp_sw = [send(v, core_swap) for v in inp_x]
    taps1, _ = lax.optimization_barrier((taps1, w2))
    w1 = rows_for_me(taps1)

    low, act_pad = low_call(at, w2, load, load_sw)
    low_x = from_x(lambda r: low)
    low_sw = [send(v, core_swap) for v in low_x]

    deep = ("zhi", "y", "zlo")
    terms1 = filter_call(-1, scale, True, at, low, inp_x, inp_sw).reshape(16, 16, 896)
    terms1 = lax.all_to_all(terms1, deep, 0, 0, tiled=True)
    terms2 = filter_call(1, scale, False, at, act_pad, load, load_sw).reshape(16, 56, 256)
    terms2 = lax.all_to_all(terms2, deep, 0, 0, tiled=True)

    bands1 = bands_call(at, w1)
    gin = input_call(at, bands1, low_x, low_sw)
    gin = jnp.stack(from_x(lambda r: gin[r])).reshape(4, 2, 192, 128)
    keep = jnp.where(first, gin[:, 0], gin[:, 1])
    away = jnp.where(first, gin[:, 1], gin[:, 0])
    gin = place_call(at, keep, send(away, core_swap))
    grad_input = gin.reshape(4, 12, 12, 256)[None]

    sum1 = terms1.astype(F32).sum(0).astype(BF)
    sum2 = terms2.astype(F32).sum(0).astype(BF)
    sum2 = send(sum2, turned)
    piece = jnp.concatenate([sum2.reshape(112, 128), sum1.reshape(112, 128)], axis=0)

    low_side = zlo == 0
    other = send(piece, zlo_swap)
    pair = jnp.stack([jnp.where(low_side, piece, other), jnp.where(low_side, other, piece)])
    xs = jnp.stack(from_x(lambda r: pair))
    xs = jnp.roll(xs, x, axis=0)
    co = send(xs, core_swap)
    all_ = jnp.stack([jnp.where(first, xs, co), jnp.where(first, co, xs)]).reshape(8, 2, 224, 128)
    out2 = all_[:, :, :112].reshape(16 * 56, 256)[:864].reshape(27, 32, 256)
    out1 = all_[:, :, 112:].reshape(8, 2, 16, 896)[..., :864].reshape(8, 32, 27, 32)
    out1 = out1.transpose(1, 2, 0, 3).reshape(32, 27, 256)
    return (grad_input, out1.astype(F32), out2.transpose(1, 0, 2).astype(F32))


def solution(mesh):
    fine = Mesh(mesh.devices.reshape(SIZES), AXES)
    dp, ty = ("zhi", "y"), ("zlo", "core")
    vol = P(dp, None, ty, "x", None)
    filt = P(dp, None, None)
    return jax.shard_map(
        local,
        mesh=fine,
        in_specs=(vol, vol, vol, vol, filt, filt),
        out_specs=(vol, filt, filt),
        check_vma=False,
    )
```
